32 devices in a mesh: wide: 8 (over y, x, core), cell: 4 (over z).
Axes of the slice: x: 2, y: 2, z: 4, core: 2. Of those that a mesh axis runs over, the one named last changes fastest.
Arguments:
- green_pair: float32 [2, 2, 32, 4, 128, 128], P(None, None, 'wide', 'cell'), may hold values from -5 to 5
- coulomb: float32 [4, 2, 128, 128], P('cell'), may hold values from -0.5 to 0.5
- green_retarded: float32 [2, 32, 4, 2, 128, 128], P(None, 'wide', 'cell'), may hold values from -0.375 to 0.375
- offsets: int32 [4, 2], P('cell'), may hold values from -1 to 1, as said below
Outputs:
- dressed: float32 [2, 32, 4, 128, 128], P(None, 'wide', 'cell')
The draws below stay inside these ranges and needn't reach their ends.
Inputs may be any that keep to these rules, and one draw needn't show every extreme that they name: Block row r stores its blocks at block columns r + offsets[r, 0] and r + offsets[r, 1], two different entries of -1, 0, 1 in increasing order. Every block row r with r even has offsets -1 and 1.
All inputs are finite; a program needn't handle non-finite values.
Results may differ from the reference program's by a relative error of at most 0.00014.
Values sent between devices are 32-bit elements; how exact they have to be, the bound alone decides.
No kernel may reach another device: no remote copies, remote signals or barrier semaphores. Data moves between devices by JAX's collectives and lax.ppermute only.
A program may use at most 64 MiB of HBM per device.

```python
import math
import jax
import jax.numpy as jnp
from jax import lax

B = 128
BR_DEV = 1
NE = 32
NB = 4


def draw_offsets(key, part):
    absent = jax.random.randint(key, (NB,), 0, 3)
    rows_all = jnp.arange(NB, dtype=jnp.int32)
    owner_even = rows_all // BR_DEV % 2 == 0
    local_place = rows_all % BR_DEV
    at_edge = jnp.logical_or(local_place == 0, local_place == BR_DEV - 1)
    forced = jnp.logical_and(owner_even, at_edge)
    absent = jnp.where(forced, 1, absent)
    below_slot = jnp.where(absent == 0, 0, -1)
    above_slot = jnp.where(absent == 2, 0, 1)
    return jnp.stack([below_slot, above_slot], axis=1).astype(jnp.int32)


def level_of(key, dims, cuts, low, high):
    factor_of, own = 1.0, jax.random.fold_in(key, 6)
    for dim, parts in cuts:
        heights = jnp.exp(jax.random.uniform(jax.random.fold_in(own, dim), (parts,), jnp.float32, low / len(cuts), high / len(cuts)))
        factor_of = factor_of * jnp.repeat(heights, dims[dim] // parts).reshape([-1 if axis == dim else 1 for axis in range(len(dims))])
    return factor_of


def bell_draw(rng, extent, deviation, most, shards=(), kind=jnp.bfloat16):
    result = jax.random.normal(rng, extent, jnp.float32) * deviation
    if len(shards) > 0:
        result = level_of(rng, extent, shards, -0.22, 0.18) * result
    return jnp.clip(result, min=-most, max=most).astype(kind)


def setup_inputs(seed: int = 0) -> dict:
    splits = jax.random.split(jax.random.key(seed), 5)
    return {
        "green_pair": bell_draw(splits[0], (2, 2, NE, NB, B, B), 0.7, 5.0, ((2, 8), (3, 4)), jnp.float32),
        "coulomb": bell_draw(splits[1], (NB, 2, B, B), B ** -0.5, 0.5, ((0, 4),), jnp.float32),
        "green_retarded": bell_draw(splits[2], (2, NE, NB, 2, B, B), (2 * B) ** -0.5, 0.375, ((1, 8), (2, 4)), jnp.float32),
        "offsets": draw_offsets(jax.random.fold_in(splits[4], 71), 0),
    }


def reference(green_pair, coulomb, green_retarded, offsets):
    period = 2 * NE
    lesser = jnp.moveaxis(green_pair[0, 0] + 1j * green_pair[0, 1], 1, 0)
    greater = jnp.moveaxis(green_pair[1, 0] + 1j * green_pair[1, 1], 1, 0)

    def polarize(couple):
        low_part, high_part = couple
        spectrum = jnp.fft.fft(low_part, period, axis=0) * jnp.fft.ifft(high_part, period, axis=0) * period
        return jnp.roll(jnp.fft.ifft(spectrum, axis=0), NE, axis=0) / math.sqrt(NE)
    polar_all = lax.map(polarize, (lesser, greater))
    polar_padded = jnp.pad(polar_all, ((1, 1), (0, 0), (0, 0), (0, 0)))

    def self_energy(block_row):
        screened = jnp.zeros((period, B, B), polar_all.dtype)
        for position in range(2):
            column = block_row + 1 + offsets[block_row, position]
            neighbour = lax.dynamic_index_in_dim(polar_padded, column, 0, keepdims=False)
            coupling = coulomb[block_row, position]
            screened = screened + jnp.einsum('ab,qbc,dc->qad', coupling, neighbour, coupling, precision=lax.Precision.HIGHEST)
        circular = jnp.roll(screened, -NE, axis=0)
        spectrum = jnp.fft.fft(lesser[block_row], period, axis=0) * jnp.fft.fft(circular, axis=0)
        return jnp.fft.ifft(spectrum, axis=0)[:NE] / math.sqrt(NE)
    rows_all = jnp.arange(NB, dtype=jnp.int32)
    sigma_all = lax.map(self_energy, rows_all)
    sigma_padded = jnp.pad(sigma_all, ((1, 1), (0, 0), (0, 0), (0, 0)))
    retarded = jnp.moveaxis(green_retarded[0] + 1j * green_retarded[1], 1, 0)

    def dressed_row(block_row):
        running = jnp.zeros((NE, B, B), sigma_all.dtype)
        for position in range(2):
            column = block_row + 1 + offsets[block_row, position]
            neighbour = lax.dynamic_index_in_dim(sigma_padded, column, 0, keepdims=False)
            green_block = retarded[block_row][:, position]
            running = running + jnp.einsum('nab,nbc,ndc->nad', green_block, neighbour, green_block, precision=lax.Precision.HIGHEST)
        return running
    dressed_all = jnp.moveaxis(lax.map(dressed_row, rows_all), 0, 1)
    return jnp.stack([dressed_all.real, dressed_all.imag]).astype(jnp.float32)
```

```python
import math

import jax
import jax.numpy as jnp
from jax import lax
from jax.experimental import pallas as pl
from jax.experimental.pallas import tpu as pltpu
from jax.sharding import PartitionSpec as P

USES_PALLAS = True
FORWARD = 3
BACKWARD = 2
HIGH = lax.Precision.HIGH
TILE = 8


def heights(order, parts):
    tiles = order // TILE
    sizes = [tiles // parts + (1 if k < tiles % parts else 0) for k in range(parts)]
    return [s * TILE for s in sizes]


def starts_of(sizes):
    return [sum(sizes[:k]) for k in range(len(sizes))]


def bits_of(peers):
    return peers.bit_length() - 1


def own_bit(me, bit):
    return (me >> bit) & 1


def spin(pair, flag, turns):
    c, s = math.cos(2 * math.pi * turns), math.sin(2 * math.pi * turns)
    on = flag == 1
    re, im = pair
    return (jnp.where(on, c * re - s * im, re), jnp.where(on, c * im + s * re, im))


def phase(me, bits, low, unit, top=0):
    pair = (jnp.float32(1.0), jnp.float32(0.0))
    if top:
        angle = 2 * math.pi * unit * (top << bits)
        pair = (jnp.float32(math.cos(angle)), jnp.float32(math.sin(angle)))
    for s in range(low):
        pair = spin(pair, own_bit(me, bits - 1 - s), unit * (1 << s))
    return pair


def times(value, c, s):
    re, im = value
    return (c * re - s * im, c * im + s * re)


def dft(values, sign):
    count = len(values)
    if count == 1:
        return values
    even, odd = dft(values[0::2], sign), dft(values[1::2], sign)
    out = [None] * count
    for k in range(count // 2):
        re, im = odd[k]
        if k == 0:
            turned = (re, im)
        elif 4 * k == count:
            turned = (-im, re) if sign > 0 else (im, -re)
        else:
            angle = sign * 2 * math.pi * k / count
            turned = times(odd[k], math.cos(angle), math.sin(angle))
        out[k] = (even[k][0] + turned[0], even[k][1] + turned[1])
        out[k + count // 2] = (even[k][0] - turned[0], even[k][1] - turned[1])
    return out


def tiles_loop(rows, step):
    def run(i, carry):
        step(pl.ds(pl.multiple_of(i * TILE, TILE), TILE))
        return carry

    lax.fori_loop(0, rows // TILE, run, 0)


def call(kernel, out_shapes, *args, smem=()):
    specs = [
        pl.BlockSpec(memory_space=pltpu.SMEM if i in smem else pltpu.VMEM)
        for i in range(len(args))
    ]
    nbytes = sum(a.size * 4 for a in args) + sum(4 * math.prod(s) for s in out_shapes)
    return pl.pallas_call(
        kernel,
        out_shape=[jax.ShapeDtypeStruct(s, jnp.float32) for s in out_shapes],
        in_specs=specs,
        out_specs=[pl.BlockSpec(memory_space=pltpu.VMEM) for _ in out_shapes],
        cost_estimate=pl.CostEstimate(flops=nbytes, bytes_accessed=nbytes, transcendentals=0),
        compiler_params=pltpu.CompilerParams(vmem_limit_bytes=nbytes + (1 << 20)),
    )(*args)


def split_first(own, got, had):
    return jnp.where(had == 1, got, own), jnp.where(had == 1, own, got)


def forward_kernel(stage, bits, own_ref, got_ref, keep_ref, send_ref):
    me = lax.axis_index("wide")
    local, rows = own_ref.shape[2], own_ref.shape[3]
    had = own_bit(me, bits - stage)
    mine = own_bit(me, bits - 1 - stage)
    c, s = phase(me, bits, stage, 1.0 / (1 << (stage + 1)))
    flip = jnp.where(mine == 1, jnp.float32(-1.0), jnp.float32(1.0))
    c, s = c * flip, s * flip

    def step(at):
        for which in range(2):
            side = -s if which == 0 else s
            for j in range(local):
                pairs = [
                    split_first(own_ref[which, i, j, at], got_ref[which, i, j, at], had)
                    for i in range(2)
                ]
                turned = times((pairs[0][1], pairs[1][1]), c, side)
                for i in range(2):
                    keep_ref[which, i, j, at] = pairs[i][0] + turned[i]
                    send_ref[which, i, j, at] = pairs[i][0] - turned[i]

    tiles_loop(rows, step)


def product_kernel(bits, own_ref, got_ref, lesser_ref, polar_ref):
    me = lax.axis_index("wide")
    local, rows = own_ref.shape[2], own_ref.shape[3]
    peers = 1 << bits
    period = 2 * peers * local
    had = own_bit(me, 0)
    c, s = phase(me, bits, bits, 1.0 / (2 * peers))
    twist = [
        [phase(me, bits, bits, j / period, top) for j in range(local)] for top in range(2)
    ]

    def step(at):
        hats = []
        for which in range(2):
            sign = -1 if which == 0 else 1
            tops = [[], []]
            for j in range(local):
                pairs = [
                    split_first(own_ref[which, i, j, at], got_ref[which, i, j, at], had)
                    for i in range(2)
                ]
                turned = times((pairs[0][1], pairs[1][1]), c, sign * s)
                for top in range(2):
                    value = tuple(
                        pairs[i][0] + turned[i] if top == 0 else pairs[i][0] - turned[i]
                        for i in range(2)
                    )
                    if j > 0:
                        value = times(value, twist[top][j][0], sign * twist[top][j][1])
                    tops[top].append(value)
            hats.append(dft(tops[0], sign) + dft(tops[1], sign))
        for f in range(2 * local):
            a, b = hats[0][f], hats[1][f]
            lesser_ref[0, f, at], lesser_ref[1, f, at] = a
            polar_ref[0, f, at], polar_ref[1, f, at] = times(a, b[0], b[1])

    tiles_loop(rows, step)


def inverse_kernel(bits, sizes, *refs):
    me = lax.axis_index("wide")
    lesser_refs, (screened_ref, keep_ref, send_ref) = refs[:-3], refs[-3:]
    local = keep_ref.shape[1]
    peers = 1 << bits
    period = 2 * peers * local
    mine = own_bit(me, 0)
    c, s = phase(me, bits, bits, 1.0 / (2 * peers))
    twist = [
        [phase(me, bits, bits, j / period, top) for j in range(local)] for top in range(2)
    ]
    for lesser_ref, start, size in zip(lesser_refs, starts_of(sizes), sizes):

        def run(k, carry, lesser_ref=lesser_ref, start=start):
            at = pl.ds(pl.multiple_of(k * TILE, TILE), TILE)
            to = pl.ds(pl.multiple_of(start + k * TILE, TILE), TILE)
            tops = []
            for top in range(2):
                values = []
                for t in range(local):
                    f = top * local + t
                    a = (lesser_ref[0, f, at], lesser_ref[1, f, at])
                    values.append(times(a, screened_ref[0, f, to], screened_ref[1, f, to]))
                values = dft(values, 1)
                tops.append(
                    [v if j == 0 else times(v, *twist[top][j]) for j, v in enumerate(values)]
                )
            for j in range(local):
                total = [tops[0][j][i] + tops[1][j][i] for i in range(2)]
                gap = times([tops[0][j][i] - tops[1][j][i] for i in range(2)], c, s)
                for i in range(2):
                    keep_ref[i, j, to] = jnp.where(mine == 1, gap[i], total[i])
                    send_ref[i, j, to] = jnp.where(mine == 1, total[i], gap[i])
            return carry

        lax.fori_loop(0, size // TILE, run, 0)


def backward_kernel(bit, bits, sizes, own_ref, got_ref, *outs):
    me = lax.axis_index("wide")
    local = own_ref.shape[1]
    had, mine = own_bit(me, bit - 1), own_bit(me, bit)
    low = bits - bit
    c, s = phase(me, bits, low, 1.0 / (1 << (low + 1)))
    for k, (start, size) in enumerate(zip(starts_of(sizes), sizes)):
        keep_ref, send_ref = outs[2 * k], outs[2 * k + 1]

        def run(i, carry, start=start, keep_ref=keep_ref, send_ref=send_ref):
            to = pl.ds(pl.multiple_of(i * TILE, TILE), TILE)
            at = pl.ds(pl.multiple_of(start + i * TILE, TILE), TILE)
            for j in range(local):
                pairs = [
                    split_first(own_ref[p, j, at], got_ref[p, j, at], had) for p in range(2)
                ]
                total = [pairs[p][0] + pairs[p][1] for p in range(2)]
                gap = times([pairs[p][0] - pairs[p][1] for p in range(2)], c, s)
                for p in range(2):
                    keep_ref[p, j, to] = jnp.where(mine == 1, gap[p], total[p])
                    send_ref[p, j, to] = jnp.where(mine == 1, total[p], gap[p])
            return carry

        lax.fori_loop(0, size // TILE, run, 0)


def add_kernel(own_ref, got_ref, out_ref):
    out_ref[...] = own_ref[...] + got_ref[...]


def chosen(slots, at_zero, at_one):
    return jnp.where(slots[0], at_zero, 0.0) + jnp.where(slots[1], at_one, 0.0)


def places_of(row):
    side = 1 - 2 * (row & 1)
    return [0, side, -side]


def prepare_coulomb(scale, offsets_ref, coulomb_ref, plain_ref, scaled_ref):
    row = lax.axis_index("cell")
    for slot, place in enumerate(places_of(row)):
        hit = [offsets_ref[0, j] == place for j in range(2)]
        value = chosen(hit, coulomb_ref[0, 0], coulomb_ref[0, 1])
        plain_ref[slot] = value
        scaled_ref[slot] = value * scale


def prepare_green(offsets_ref, green_ref, out_ref):
    row = lax.axis_index("cell")
    local, order = green_ref.shape[1], green_ref.shape[-1]
    for slot, place in enumerate(places_of(row)):
        hit = [offsets_ref[0, j] == place for j in range(2)]
        for e in range(local):
            re, im = (chosen(hit, green_ref[i, e, 0, 0], green_ref[i, e, 0, 1]) for i in range(2))
            out_ref[slot, e, :order, :order] = re
            out_ref[slot, e, :order, order:] = -im
            out_ref[slot, e, order:, :order] = im
            out_ref[slot, e, order:, order:] = re


def congruence(left, middle):
    order = middle.shape[-1]
    stacked = jnp.concatenate([middle[0], middle[1]], axis=-2)
    half = jnp.einsum("eab,ebc->eac", left, stacked, precision=HIGH)
    flat = jnp.concatenate([half[:, :order], half[:, order:]], axis=-1)
    out = jnp.einsum("eab,ecb->eac", flat, left, precision=HIGH)
    return jnp.stack([out[..., :order], out[..., order:]])


def body(green_pair, coulomb, green_retarded, offsets):
    peers, cells = lax.axis_size("wide"), lax.axis_size("cell")
    local, order = green_pair.shape[2], green_pair.shape[-1]
    bits = bits_of(peers)
    energies = peers * local
    scale = 1.0 / (2 * energies * energies)

    def swap(value, bit):
        return lax.ppermute(value, "wide", [(i, i ^ (1 << bit)) for i in range(peers)])

    links = []
    for first in range(2):
        up = [(i, i + 1) for i in range(first, cells - 1, 2)]
        links.append(up + [(j, i) for i, j in up])

    def beside(value):
        return [lax.ppermute(value, "cell", pairs) for pairs in links]

    pair = green_pair[:, :, :, 0]
    sizes = heights(order, FORWARD)
    keep = [
        lax.slice_in_dim(pair, at, at + size, axis=3) for at, size in zip(starts_of(sizes), sizes)
    ]
    got = [swap(k, bits - 1) for k in keep]
    plain, scaled = call(
        lambda *refs: prepare_coulomb(scale, *refs),
        [(3, order, order)] * 2, offsets, coulomb, smem=(0,),
    )
    left, = call(prepare_green, [(3, local, 2 * order, 2 * order)], offsets, green_retarded, smem=(0,))
    for stage in range(1, bits):
        for k in range(FORWARD):
            keep[k], send = call(
                lambda *refs: forward_kernel(stage, bits, *refs), [keep[k].shape] * 2, keep[k], got[k]
            )
            got[k] = swap(send, bits - 1 - stage)
    lesser, polar, near = [], [], []
    for k, size in enumerate(sizes):
        hat, product = call(
            lambda *refs: product_kernel(bits, *refs),
            [(2, 2 * local, size, order)] * 2, keep[k], got[k],
        )
        lesser.append(hat)
        polar.append(product)
        near.append([product] + beside(product))

    screened = 0.0
    for slot in range(3):
        whole = jnp.concatenate([n[slot] for n in near], axis=2)
        half = jnp.einsum("pfbc,dc->pfbd", whole, scaled[slot], precision=HIGH)
        screened = screened + jnp.einsum("ab,pfbd->pfad", plain[slot], half, precision=HIGH)

    keep, send = call(
        lambda *refs: inverse_kernel(bits, sizes, *refs),
        [(2, local, order, order)] * 2, *lesser, screened,
    )
    got = swap(send, 0)
    sizes = heights(order, BACKWARD)
    outs = call(
        lambda *refs: backward_kernel(1, bits, sizes, *refs),
        [(2, local, size, order) for size in sizes for _ in range(2)], keep, got,
    )
    keep, got = list(outs[0::2]), [swap(s, 1) for s in outs[1::2]]
    for bit in range(2, bits):
        for k, size in enumerate(sizes):
            keep[k], send = call(
                lambda *refs: backward_kernel(bit, bits, [size], *refs),
                [keep[k].shape] * 2, keep[k], got[k],
            )
            got[k] = swap(send, bit)
    near = []
    for k, size in enumerate(sizes):
        sigma, = call(add_kernel, [keep[k].shape], keep[k], got[k])
        near.append([sigma] + beside(sigma))
    result = 0.0
    for slot in range(3):
        middle = jnp.concatenate([n[slot] for n in near], axis=2)
        result = result + congruence(left[slot], middle)
    return result[:, :, None]


def solution(mesh):
    placed = (
        P(None, None, "wide", "cell", None, None),
        P("cell", None, None, None),
        P(None, "wide", "cell", None, None, None),
        P("cell", None),
    )
    return jax.shard_map(
        body,
        mesh=mesh,
        in_specs=placed,
        out_specs=P(None, "wide", "cell", None, None),
        check_vma=False,
    )
```

```python
from functools import partial
import math

import jax
import jax.numpy as jnp
from jax import lax
from jax.experimental import pallas as pl
from jax.experimental.pallas import tpu as pltpu
from jax.sharding import PartitionSpec as P


FORWARD = 3
BACKWARD = 2
HIGH = lax.Precision.HIGH
TILE = 8


def heights(order, parts):
    tiles = order // TILE
    sizes = [tiles // parts + (1 if k < tiles % parts else 0) for k in range(parts)]
    return [s * TILE for s in sizes]


def starts_of(sizes):
    return [sum(sizes[:k]) for k in range(len(sizes))]


def waves(parts, stages):
    pairs = [(k, stage) for k in range(parts) for stage in stages]
    return sorted(pairs, key=lambda p: (p[0] + p[1], p[1]))


def bits_of(peers):
    return peers.bit_length() - 1


def own_bit(me, bit):
    return (me >> bit) & 1


def spin(pair, flag, turns):
    c, s = math.cos(2 * math.pi * turns), math.sin(2 * math.pi * turns)
    on = flag == 1
    re, im = pair
    return (jnp.where(on, c * re - s * im, re), jnp.where(on, c * im + s * re, im))


def phase(me, bits, low, unit, top=0):
    pair = (jnp.float32(1.0), jnp.float32(0.0))
    if top:
        angle = 2 * math.pi * unit * (top << bits)
        pair = (jnp.float32(math.cos(angle)), jnp.float32(math.sin(angle)))
    for s in range(low):
        pair = spin(pair, own_bit(me, bits - 1 - s), unit * (1 << s))
    return pair


def times(value, c, s):
    re, im = value
    return (c * re - s * im, c * im + s * re)


def dft(values, sign):
    count = len(values)
    if count == 1:
        return values
    even, odd = dft(values[0::2], sign), dft(values[1::2], sign)
    out = [None] * count
    for k in range(count // 2):
        re, im = odd[k]
        if k == 0:
            turned = (re, im)
        elif 4 * k == count:
            turned = (-im, re) if sign > 0 else (im, -re)
        else:
            angle = sign * 2 * math.pi * k / count
            turned = times(odd[k], math.cos(angle), math.sin(angle))
        out[k] = (even[k][0] + turned[0], even[k][1] + turned[1])
        out[k + count // 2] = (even[k][0] - turned[0], even[k][1] - turned[1])
    return out


def tiles_loop(rows, step):
    def run(i, carry):
        step(pl.ds(pl.multiple_of(i * TILE, TILE), TILE))
        return carry

    lax.fori_loop(0, rows // TILE, run, 0)


def call(kernel, out_shapes, *args, smem=()):
    specs = [
        pl.BlockSpec(memory_space=pltpu.SMEM if i in smem else pltpu.VMEM)
        for i in range(len(args))
    ]
    nbytes = sum(a.size * 4 for a in args) + sum(4 * math.prod(s) for s in out_shapes)
    return pl.pallas_call(
        kernel,
        out_shape=[jax.ShapeDtypeStruct(s, jnp.float32) for s in out_shapes],
        in_specs=specs,
        out_specs=[pl.BlockSpec(memory_space=pltpu.VMEM) for _ in out_shapes],
        cost_estimate=pl.CostEstimate(flops=nbytes, bytes_accessed=nbytes, transcendentals=0),
        compiler_params=pltpu.CompilerParams(vmem_limit_bytes=nbytes + (1 << 20)),
    )(*args)


def split_first(own, got, had):
    return jnp.where(had == 1, got, own), jnp.where(had == 1, own, got)


def forward_kernel(stage, bits, own_ref, got_ref, keep_ref, send_ref):
    me = lax.axis_index("wide")
    local, rows = own_ref.shape[2], own_ref.shape[3]
    had = own_bit(me, bits - stage)
    mine = own_bit(me, bits - 1 - stage)
    c, s = phase(me, bits, stage, 1.0 / (1 << (stage + 1)))
    flip = jnp.where(mine == 1, jnp.float32(-1.0), jnp.float32(1.0))
    c, s = c * flip, s * flip

    def step(at):
        for which in range(2):
            side = -s if which == 0 else s
            for j in range(local):
                pairs = [
                    split_first(own_ref[which, i, j, at], got_ref[which, i, j, at], had)
                    for i in range(2)
                ]
                turned = times((pairs[0][1], pairs[1][1]), c, side)
                for i in range(2):
                    keep_ref[which, i, j, at] = pairs[i][0] + turned[i]
                    send_ref[which, i, j, at] = pairs[i][0] - turned[i]

    tiles_loop(rows, step)


def product_kernel(bits, own_ref, got_ref, lesser_ref, polar_ref):
    me = lax.axis_index("wide")
    local, rows = own_ref.shape[2], own_ref.shape[3]
    peers = 1 << bits
    period = 2 * peers * local
    had = own_bit(me, 0)
    c, s = phase(me, bits, bits, 1.0 / (2 * peers))
    twist = [
        [phase(me, bits, bits, j / period, top) for j in range(local)] for top in range(2)
    ]

    def step(at):
        hats = []
        for which in range(2):
            sign = -1 if which == 0 else 1
            tops = [[], []]
            for j in range(local):
                pairs = [
                    split_first(own_ref[which, i, j, at], got_ref[which, i, j, at], had)
                    for i in range(2)
                ]
                turned = times((pairs[0][1], pairs[1][1]), c, sign * s)
                for top in range(2):
                    value = tuple(
                        pairs[i][0] + turned[i] if top == 0 else pairs[i][0] - turned[i]
                        for i in range(2)
                    )
                    if j > 0:
                        value = times(value, twist[top][j][0], sign * twist[top][j][1])
                    tops[top].append(value)
            hats.append(dft(tops[0], sign) + dft(tops[1], sign))
        for f in range(2 * local):
            a, b = hats[0][f], hats[1][f]
            lesser_ref[0, f, at], lesser_ref[1, f, at] = a
            polar_ref[0, f, at], polar_ref[1, f, at] = times(a, b[0], b[1])

    tiles_loop(rows, step)


def inverse_kernel(bits, sizes, *refs):
    me = lax.axis_index("wide")
    lesser_refs, (screened_ref, keep_ref, send_ref) = refs[:-3], refs[-3:]
    local = keep_ref.shape[1]
    peers = 1 << bits
    period = 2 * peers * local
    mine = own_bit(me, 0)
    c, s = phase(me, bits, bits, 1.0 / (2 * peers))
    twist = [
        [phase(me, bits, bits, j / period, top) for j in range(local)] for top in range(2)
    ]
    for lesser_ref, start, size in zip(lesser_refs, starts_of(sizes), sizes):

        def run(k, carry, lesser_ref=lesser_ref, start=start):
            at = pl.ds(pl.multiple_of(k * TILE, TILE), TILE)
            to = pl.ds(pl.multiple_of(start + k * TILE, TILE), TILE)
            tops = []
            for top in range(2):
                values = []
                for t in range(local):
                    f = top * local + t
                    a = (lesser_ref[0, f, at], lesser_ref[1, f, at])
                    values.append(times(a, screened_ref[0, f, to], screened_ref[1, f, to]))
                values = dft(values, 1)
                tops.append(
                    [v if j == 0 else times(v, *twist[top][j]) for j, v in enumerate(values)]
                )
            for j in range(local):
                total = [tops[0][j][i] + tops[1][j][i] for i in range(2)]
                gap = times([tops[0][j][i] - tops[1][j][i] for i in range(2)], c, s)
                for i in range(2):
                    keep_ref[i, j, to] = jnp.where(mine == 1, gap[i], total[i])
                    send_ref[i, j, to] = jnp.where(mine == 1, total[i], gap[i])
            return carry

        lax.fori_loop(0, size // TILE, run, 0)


def backward_kernel(bit, bits, sizes, own_ref, got_ref, *outs):
    me = lax.axis_index("wide")
    local = own_ref.shape[1]
    had, mine = own_bit(me, bit - 1), own_bit(me, bit)
    low = bits - bit
    c, s = phase(me, bits, low, 1.0 / (1 << (low + 1)))
    for k, (start, size) in enumerate(zip(starts_of(sizes), sizes)):
        keep_ref, send_ref = outs[2 * k], outs[2 * k + 1]

        def run(i, carry, start=start, keep_ref=keep_ref, send_ref=send_ref):
            to = pl.ds(pl.multiple_of(i * TILE, TILE), TILE)
            at = pl.ds(pl.multiple_of(start + i * TILE, TILE), TILE)
            for j in range(local):
                pairs = [
                    split_first(own_ref[p, j, at], got_ref[p, j, at], had) for p in range(2)
                ]
                total = [pairs[p][0] + pairs[p][1] for p in range(2)]
                gap = times([pairs[p][0] - pairs[p][1] for p in range(2)], c, s)
                for p in range(2):
                    keep_ref[p, j, to] = jnp.where(mine == 1, gap[p], total[p])
                    send_ref[p, j, to] = jnp.where(mine == 1, total[p], gap[p])
            return carry

        lax.fori_loop(0, size // TILE, run, 0)


def add_kernel(own_ref, got_ref, out_ref):
    out_ref[...] = own_ref[...] + got_ref[...]


def chosen(slots, at_zero, at_one):
    return jnp.where(slots[0], at_zero, 0.0) + jnp.where(slots[1], at_one, 0.0)


def places_of(row):
    side = 1 - 2 * (row & 1)
    return [0, side, -side]


def prepare_coulomb(scale, offsets_ref, coulomb_ref, plain_ref, scaled_ref):
    row = lax.axis_index("cell")
    for slot, place in enumerate(places_of(row)):
        hit = [offsets_ref[0, j] == place for j in range(2)]
        value = chosen(hit, coulomb_ref[0, 0], coulomb_ref[0, 1])
        plain_ref[slot] = value
        scaled_ref[slot] = value * scale


def prepare_green(offsets_ref, green_ref, out_ref):
    row = lax.axis_index("cell")
    local, order = green_ref.shape[1], green_ref.shape[-1]
    for slot, place in enumerate(places_of(row)):
        hit = [offsets_ref[0, j] == place for j in range(2)]
        for e in range(local):
            re, im = (chosen(hit, green_ref[i, e, 0, 0], green_ref[i, e, 0, 1]) for i in range(2))
            out_ref[slot, e, :order, :order] = re
            out_ref[slot, e, :order, order:] = -im
            out_ref[slot, e, order:, :order] = im
            out_ref[slot, e, order:, order:] = re


def congruence(left, middle):
    order = middle.shape[-1]
    stacked = jnp.concatenate([middle[0], middle[1]], axis=-2)
    half = jnp.einsum("eab,ebc->eac", left, stacked, precision=HIGH)
    flat = jnp.concatenate([half[:, :order], half[:, order:]], axis=-1)
    out = jnp.einsum("eab,ecb->eac", flat, left, precision=HIGH)
    return jnp.stack([out[..., :order], out[..., order:]])


def body(green_pair, coulomb, green_retarded, offsets):
    peers, cells = lax.axis_size("wide"), lax.axis_size("cell")
    local, order = green_pair.shape[2], green_pair.shape[-1]
    bits = bits_of(peers)
    energies = peers * local
    scale = 1.0 / (2 * energies * energies)

    def swap(value, bit):
        return lax.ppermute(value, "wide", [(i, i ^ (1 << bit)) for i in range(peers)])

    links = []
    for first in range(2):
        up = [(i, i + 1) for i in range(first, cells - 1, 2)]
        links.append(up + [(j, i) for i, j in up])

    def beside(value):
        blocks = []
        for pairs in links:
            blocks.append(lax.ppermute(value, "cell", pairs))
        return blocks

    pair = green_pair[:, :, :, 0]
    sizes = heights(order, FORWARD)
    keep = [
        lax.slice_in_dim(pair, at, at + size, axis=3) for at, size in zip(starts_of(sizes), sizes)
    ]
    got = [swap(own, bits - 1) for own in keep]
    plain, scaled = call(
        partial(prepare_coulomb, scale),
        [(3, order, order)] * 2, offsets, coulomb, smem=(0,),
    )
    left, = call(
        prepare_green, [(3, local, 2 * order, 2 * order)],
        offsets, green_retarded, smem=(0,),
    )
    lesser, near = [None] * FORWARD, [None] * FORWARD
    for k, stage in waves(FORWARD, range(1, bits)):
        keep[k], send = call(
            partial(forward_kernel, stage, bits),
            [keep[k].shape] * 2, keep[k], got[k],
        )
        got[k] = swap(send, bits - 1 - stage)
        if stage == bits - 1:
            lesser[k], polar = call(
                partial(product_kernel, bits),
                [(2, 2 * local, sizes[k], order)] * 2, keep[k], got[k],
            )
            near[k] = [polar] + beside(polar)

    screened = 0.0
    for slot in range(3):
        whole = jnp.concatenate([n[slot] for n in near], axis=2)
        half = jnp.einsum("pfbc,dc->pfbd", whole, scaled[slot], precision=HIGH)
        screened = screened + jnp.einsum("ab,pfbd->pfad", plain[slot], half, precision=HIGH)

    keep, send = call(
        partial(inverse_kernel, bits, sizes),
        [(2, local, order, order)] * 2, *lesser, screened,
    )
    got = swap(send, 0)
    sizes = heights(order, BACKWARD)
    outs = call(
        partial(backward_kernel, 1, bits, sizes),
        [(2, local, size, order) for size in sizes for _ in range(2)], keep, got,
    )
    keep = list(outs[0::2])
    got = [swap(send, 1) for send in outs[1::2]]
    near = [None] * BACKWARD
    for k, bit in waves(BACKWARD, range(2, bits + 1)):
        if bit < bits:
            keep[k], send = call(
                partial(backward_kernel, bit, bits, [sizes[k]]),
                [keep[k].shape] * 2, keep[k], got[k],
            )
            got[k] = swap(send, bit)
        else:
            sigma, = call(add_kernel, [keep[k].shape], keep[k], got[k])
            near[k] = [sigma] + beside(sigma)
    result = 0.0
    for slot in range(3):
        middle = jnp.concatenate([n[slot] for n in near], axis=2)
        result = result + congruence(left[slot], middle)
    return result[:, :, None]


def solution(mesh):
    placed = (
        P(None, None, "wide", "cell", None, None),
        P("cell", None, None, None),
        P(None, "wide", "cell", None, None, None),
        P("cell", None),
    )

    return jax.shard_map(
        body,
        mesh=mesh,
        in_specs=placed,
        out_specs=P(None, "wide", "cell", None, None),
        check_vma=False,
    )
```

```python
from functools import partial
import math

import jax
import jax.numpy as jnp
from jax import lax
from jax.experimental import pallas as pl
from jax.experimental.pallas import tpu as pltpu
from jax.sharding import PartitionSpec as P


FORWARD = 4
BACKWARD = 3
TILE = 8
GRAIN = 16


def heights(order, parts):
    grains = order // GRAIN
    sizes = [grains // parts + (1 if k < grains % parts else 0) for k in range(parts)]
    return [s * GRAIN for s in sizes]


def starts_of(sizes):
    return [sum(sizes[:k]) for k in range(len(sizes))]


def waves(parts, stages):
    pairs = [(k, stage) for k in range(parts) for stage in stages]
    return sorted(pairs, key=lambda p: (p[0] + p[1], p[1]))


def bits_of(peers):
    return peers.bit_length() - 1


def own_bit(me, bit):
    return (me >> bit) & 1


def spin(pair, flag, turns):
    c, s = math.cos(2 * math.pi * turns), math.sin(2 * math.pi * turns)
    on = flag == 1
    re, im = pair
    return (jnp.where(on, c * re - s * im, re), jnp.where(on, c * im + s * re, im))


def phase(me, bits, low, unit, top=0):
    pair = (jnp.float32(1.0), jnp.float32(0.0))
    if top:
        angle = 2 * math.pi * unit * (top << bits)
        pair = (jnp.float32(math.cos(angle)), jnp.float32(math.sin(angle)))
    for s in range(low):
        pair = spin(pair, own_bit(me, bits - 1 - s), unit * (1 << s))
    return pair


def times(value, c, s):
    re, im = value
    return (c * re - s * im, c * im + s * re)


def dft(values, sign):
    count = len(values)
    if count == 1:
        return values
    even, odd = dft(values[0::2], sign), dft(values[1::2], sign)
    out = [None] * count
    for k in range(count // 2):
        re, im = odd[k]
        if k == 0:
            turned = (re, im)
        elif 4 * k == count:
            turned = (-im, re) if sign > 0 else (im, -re)
        else:
            angle = sign * 2 * math.pi * k / count
            turned = times(odd[k], math.cos(angle), math.sin(angle))
        out[k] = (even[k][0] + turned[0], even[k][1] + turned[1])
        out[k + count // 2] = (even[k][0] - turned[0], even[k][1] - turned[1])
    return out


def tiles_loop(rows, step):
    def run(i, carry):
        step(pl.ds(pl.multiple_of(i * TILE, TILE), TILE))
        return carry

    lax.fori_loop(0, rows // TILE, run, 0)


def call(kernel, outs, *args, smem=(), scratch=(), alias=None):
    specs = [
        pl.BlockSpec(memory_space=pltpu.SMEM if i in smem else pltpu.VMEM)
        for i in range(len(args))
    ]
    outs = [o if isinstance(o, jax.ShapeDtypeStruct) else full(o) for o in outs]
    nbytes = sum(a.size * a.dtype.itemsize for a in [*args, *outs, *map(full, scratch)])
    return pl.pallas_call(
        kernel,
        out_shape=outs,
        in_specs=specs,
        out_specs=[pl.BlockSpec(memory_space=pltpu.VMEM) for _ in outs],
        scratch_shapes=[pltpu.VMEM(shape, jnp.float32) for shape in scratch],
        input_output_aliases=alias or {},
        cost_estimate=pl.CostEstimate(flops=nbytes, bytes_accessed=nbytes, transcendentals=0),
        compiler_params=pltpu.CompilerParams(vmem_limit_bytes=nbytes + (4 << 20)),
    )(*args)


def full(shape):
    return jax.ShapeDtypeStruct(shape, jnp.float32)


def half(shape):
    return jax.ShapeDtypeStruct(shape, jnp.bfloat16)


def halves(value):
    high = value.astype(jnp.bfloat16)
    return high, (value - high.astype(jnp.float32)).astype(jnp.bfloat16)


def product_of(left, right):
    dot = partial(jnp.dot, preferred_element_type=jnp.float32)
    return dot(left[0], right[0]) + (dot(left[0], right[1]) + dot(left[1], right[0]))


def split_first(own, got, had):
    return jnp.where(had == 1, got, own), jnp.where(had == 1, own, got)


def forward_kernel(stage, bits, own_ref, got_ref, keep_ref, send_ref):
    me = lax.axis_index("wide")
    local, rows = own_ref.shape[2], own_ref.shape[3]
    had = own_bit(me, bits - stage)
    mine = own_bit(me, bits - 1 - stage)
    c, s = phase(me, bits, stage, 1.0 / (1 << (stage + 1)))
    flip = jnp.where(mine == 1, jnp.float32(-1.0), jnp.float32(1.0))
    c, s = c * flip, s * flip

    def step(at):
        for which in range(2):
            side = -s if which == 0 else s
            for j in range(local):
                pairs = [
                    split_first(own_ref[which, i, j, at], got_ref[which, i, j, at], had)
                    for i in range(2)
                ]
                turned = times((pairs[0][1], pairs[1][1]), c, side)
                for i in range(2):
                    keep_ref[which, i, j, at] = pairs[i][0] + turned[i]
                    send_ref[which, i, j, at] = pairs[i][0] - turned[i]

    tiles_loop(rows, step)


def product_kernel(bits, own_ref, got_ref, lesser_ref, polar_ref):
    me = lax.axis_index("wide")
    local, rows = own_ref.shape[2], own_ref.shape[3]
    peers = 1 << bits
    period = 2 * peers * local
    had = own_bit(me, 0)
    c, s = phase(me, bits, bits, 1.0 / (2 * peers))
    twist = [
        [phase(me, bits, bits, j / period, top) for j in range(local)] for top in range(2)
    ]

    def step(at):
        hats = []
        for which in range(2):
            sign = -1 if which == 0 else 1
            tops = [[], []]
            for j in range(local):
                pairs = [
                    split_first(own_ref[which, i, j, at], got_ref[which, i, j, at], had)
                    for i in range(2)
                ]
                turned = times((pairs[0][1], pairs[1][1]), c, sign * s)
                for top in range(2):
                    value = tuple(
                        pairs[i][0] + turned[i] if top == 0 else pairs[i][0] - turned[i]
                        for i in range(2)
                    )
                    if j > 0:
                        value = times(value, twist[top][j][0], sign * twist[top][j][1])
                    tops[top].append(value)
            hats.append(dft(tops[0], sign) + dft(tops[1], sign))
        for f in range(2 * local):
            a, b = hats[0][f], hats[1][f]
            lesser_ref[0, f, at], lesser_ref[1, f, at] = a
            polar_ref[0, f, at], polar_ref[1, f, at] = times(a, b[0], b[1])

    tiles_loop(rows, step)


def backward_kernel(bit, bits, sizes, own_ref, got_ref, *outs):
    me = lax.axis_index("wide")
    local = own_ref.shape[1]
    had, mine = own_bit(me, bit - 1), own_bit(me, bit)
    low = bits - bit
    c, s = phase(me, bits, low, 1.0 / (1 << (low + 1)))
    for k, (start, size) in enumerate(zip(starts_of(sizes), sizes)):
        keep_ref, send_ref = outs[2 * k], outs[2 * k + 1]

        def run(i, carry, start=start, keep_ref=keep_ref, send_ref=send_ref):
            to = pl.ds(pl.multiple_of(i * TILE, TILE), TILE)
            at = pl.ds(pl.multiple_of(start + i * TILE, TILE), TILE)
            for j in range(local):
                pairs = [
                    split_first(own_ref[p, j, at], got_ref[p, j, at], had) for p in range(2)
                ]
                total = [pairs[p][0] + pairs[p][1] for p in range(2)]
                gap = times([pairs[p][0] - pairs[p][1] for p in range(2)], c, s)
                for p in range(2):
                    keep_ref[p, j, to] = jnp.where(mine == 1, gap[p], total[p])
                    send_ref[p, j, to] = jnp.where(mine == 1, total[p], gap[p])
            return carry

        lax.fori_loop(0, size // TILE, run, 0)


def add_kernel(own_ref, got_ref, out_ref):
    out_ref[...] = own_ref[...] + got_ref[...]


def chosen(slots, at_zero, at_one):
    return jnp.where(slots[0], at_zero, 0.0) + jnp.where(slots[1], at_one, 0.0)


def places_of(row):
    side = 1 - 2 * (row & 1)
    return [0, side, -side]


def prepare_coulomb(scale, offsets_ref, coulomb_ref, left_high, left_low, right_high, right_low):
    row = lax.axis_index("cell")
    order = coulomb_ref.shape[-1]
    for slot, place in enumerate(places_of(row)):
        hit = [offsets_ref[0, j] == place for j in range(2)]
        value = chosen(hit, coulomb_ref[0, 0], coulomb_ref[0, 1])
        at = slice(slot * order, (slot + 1) * order)
        left_high[:, at], left_low[:, at] = halves(value)
        right_high[slot], right_low[slot] = halves(value.T * scale)


def prepare_green(offsets_ref, green_ref, left_high, left_low, right_high, right_low):
    row = lax.axis_index("cell")
    local, order = green_ref.shape[1], green_ref.shape[-1]
    low, top = slice(0, order), slice(order, 2 * order)
    for slot, place in enumerate(places_of(row)):
        hit = [offsets_ref[0, j] == place for j in range(2)]
        for e in range(local):
            parts = [chosen(hit, green_ref[i, e, 0, 0], green_ref[i, e, 0, 1]) for i in range(2)]
            re, im = (halves(p) for p in parts)
            re_t, im_t = (halves(p.T) for p in parts)
            for i, (left, right) in enumerate(((left_high, right_high), (left_low, right_low))):
                left[slot, e, low, low], left[slot, e, top, top] = re[i], re[i]
                left[slot, e, low, top], left[slot, e, top, low] = -im[i], im[i]
                right[slot, e, low, low], right[slot, e, top, top] = re_t[i], re_t[i]
                right[slot, e, top, low], right[slot, e, low, top] = -im_t[i], im_t[i]


def screen_kernel(start, *refs):
    blocks, (right_high, right_low), (out_high, out_low) = refs[:3], refs[3:5], refs[-2:]
    count, rows, order = blocks[0].shape[1], blocks[0].shape[2], blocks[0].shape[3]
    for slot, ref in enumerate(blocks):
        value = halves(ref[...].reshape(2 * count * rows, order))
        result = halves(product_of(value, (right_high[slot], right_low[slot])))
        at = slice(slot * order + start, slot * order + start + rows)
        for i, out in enumerate((out_high, out_low)):
            out[:, :, at] = result[i].reshape(2, count, rows, order)


def inverse_kernel(bits, sizes, *refs):
    me = lax.axis_index("wide")
    lesser_refs, refs = refs[: len(sizes)], refs[len(sizes) :]
    left_high, left_low, mid_high, mid_low, keep_ref, send_ref, screened = refs
    for i in range(2):
        for f in range(mid_high.shape[1]):
            screened[i, f] = product_of(
                (left_high[...], left_low[...]), (mid_high[i, f], mid_low[i, f])
            )
    local = keep_ref.shape[1]
    peers = 1 << bits
    period = 2 * peers * local
    mine = own_bit(me, 0)
    c, s = phase(me, bits, bits, 1.0 / (2 * peers))
    twist = [
        [phase(me, bits, bits, j / period, top) for j in range(local)] for top in range(2)
    ]
    for lesser_ref, start, size in zip(lesser_refs, starts_of(sizes), sizes):

        def run(k, carry, lesser_ref=lesser_ref, start=start):
            at = pl.ds(pl.multiple_of(k * TILE, TILE), TILE)
            to = pl.ds(pl.multiple_of(start + k * TILE, TILE), TILE)
            tops = []
            for top in range(2):
                values = []
                for t in range(local):
                    f = top * local + t
                    a = (lesser_ref[0, f, at], lesser_ref[1, f, at])
                    values.append(times(a, screened[0, f, to], screened[1, f, to]))
                values = dft(values, 1)
                tops.append(
                    [v if j == 0 else times(v, *twist[top][j]) for j, v in enumerate(values)]
                )
            for j in range(local):
                total = [tops[0][j][i] + tops[1][j][i] for i in range(2)]
                gap = times([tops[0][j][i] - tops[1][j][i] for i in range(2)], c, s)
                for i in range(2):
                    keep_ref[i, j, to] = jnp.where(mine == 1, gap[i], total[i])
                    send_ref[i, j, to] = jnp.where(mine == 1, total[i], gap[i])
            return carry

        lax.fori_loop(0, size // TILE, run, 0)


def times_right(block_ref, e, right_high, right_low, slot):
    value = halves(jnp.concatenate([block_ref[0, e], block_ref[1, e]], axis=-1))
    return product_of(value, (right_high[slot, e], right_low[slot, e]))


def own_dressing_kernel(count, *refs):
    blocks, (left_high, left_low, right_high, right_low, out_ref) = refs[:count], refs[count:]
    local, order = out_ref.shape[1], out_ref.shape[-1]
    for e in range(local):
        parts = [times_right(b, e, right_high, right_low, 0) for b in blocks]
        middle = jnp.concatenate(
            [p[:, :order] for p in parts] + [p[:, order:] for p in parts], axis=0
        )
        out = product_of((left_high[0, e], left_low[0, e]), halves(middle))
        out_ref[0, e], out_ref[1, e] = out[:order], out[order:]


def dress_kernel(start, *refs):
    blocks, (right_high, right_low), (out_high, out_low) = refs[:2], refs[2:4], refs[-2:]
    local, rows, order = blocks[0].shape[1], blocks[0].shape[2], blocks[0].shape[3]
    for slot, ref in enumerate(blocks):
        for e in range(local):
            result = halves(times_right(ref, e, right_high, right_low, slot + 1))
            for p in range(2):
                to = slice((2 * slot + p) * order + start, (2 * slot + p) * order + start + rows)
                at = slice(p * order, (p + 1) * order)
                out_high[e, to], out_low[e, to] = result[0][:, at], result[1][:, at]


def finish_kernel(own_ref, left_high, left_low, mid_high, mid_low, out_ref):
    local, order = out_ref.shape[1], out_ref.shape[-1]
    for e in range(local):
        total = 0.0
        for slot in range(2):
            at = slice(2 * slot * order, 2 * (slot + 1) * order)
            total = total + product_of(
                (left_high[slot + 1, e], left_low[slot + 1, e]), (mid_high[e, at], mid_low[e, at])
            )
        out_ref[0, e, 0] = own_ref[0, e] + total[:order]
        out_ref[1, e, 0] = own_ref[1, e] + total[order:]


def body(green_pair, coulomb, green_retarded, offsets):
    peers, cells = lax.axis_size("wide"), lax.axis_size("cell")
    local, order = green_pair.shape[2], green_pair.shape[-1]
    bits = bits_of(peers)
    energies = peers * local
    scale = 1.0 / (2 * energies * energies)

    def swap(value, bit):
        return lax.ppermute(value, "wide", [(i, i ^ (1 << bit)) for i in range(peers)])

    links = []
    for first in range(2):
        up = [(i, i + 1) for i in range(first, cells - 1, 2)]
        links.append(up + [(j, i) for i, j in up])

    def beside(value):
        blocks = []
        for pairs in links:
            blocks.append(lax.ppermute(value, "cell", pairs))
        return blocks

    pair = green_pair[:, :, :, 0]
    sizes = heights(order, FORWARD)
    keep = [
        lax.slice_in_dim(pair, at, at + size, axis=3) for at, size in zip(starts_of(sizes), sizes)
    ]
    got = [swap(own, bits - 1) for own in keep]
    coulomb_shapes = [(order, 3 * order)] * 2 + [(3, order, order)] * 2
    coulombs = call(
        partial(prepare_coulomb, scale), [half(c) for c in coulomb_shapes],
        offsets, coulomb, smem=(0,),
    )
    greens = call(
        prepare_green, [half((3, local, 2 * order, 2 * order))] * 4,
        offsets, green_retarded, smem=(0,),
    )
    lesser, near = [None] * FORWARD, [None] * FORWARD
    for k, stage in waves(FORWARD, range(1, bits)):
        keep[k], send = call(
            partial(forward_kernel, stage, bits),
            [keep[k].shape] * 2, keep[k], got[k],
        )
        got[k] = swap(send, bits - 1 - stage)
        if stage == bits - 1:
            lesser[k], polar = call(
                partial(product_kernel, bits),
                [(2, 2 * local, sizes[k], order)] * 2, keep[k], got[k],
            )
            near[k] = [polar] + beside(polar)

    middle = []
    for k, start in enumerate(starts_of(sizes)):
        middle = call(
            partial(screen_kernel, start),
            [half((2, 2 * local, 3 * order, order))] * 2, *near[k], *coulombs[2:], *middle,
            alias={5: 0, 6: 1} if k else None,
        )
    keep, send = call(
        partial(inverse_kernel, bits, sizes),
        [(2, local, order, order)] * 2, *lesser, *coulombs[:2], *middle,
        scratch=[(2, 2 * local, order, order)],
    )
    got = swap(send, 0)
    sizes = heights(order, BACKWARD)
    outs = call(
        partial(backward_kernel, 1, bits, sizes),
        [(2, local, size, order) for size in sizes for _ in range(2)], keep, got,
    )
    keep = list(outs[0::2])
    got = [swap(send, 1) for send in outs[1::2]]
    near = [None] * BACKWARD
    for k, bit in waves(BACKWARD, range(2, bits + 1)):
        if bit < bits:
            keep[k], send = call(
                partial(backward_kernel, bit, bits, [sizes[k]]),
                [keep[k].shape] * 2, keep[k], got[k],
            )
            got[k] = swap(send, bit)
        else:
            sigma, = call(add_kernel, [keep[k].shape], keep[k], got[k])
            near[k] = [sigma] + beside(sigma)
    own, = call(
        partial(own_dressing_kernel, BACKWARD), [(2, local, order, order)],
        *[n[0] for n in near], *greens,
    )
    middle = []
    for k, start in enumerate(starts_of(sizes)):
        middle = call(
            partial(dress_kernel, start), [half((local, 4 * order, order))] * 2,
            *near[k][1:], *greens[2:], *middle, alias={4: 0, 5: 1} if k else None,
        )
    result, = call(finish_kernel, [(2, local, 1, order, order)], own, *greens[:2], *middle)
    return result


def solution(mesh):
    placed = (
        P(None, None, "wide", "cell", None, None),
        P("cell", None, None, None),
        P(None, "wide", "cell", None, None, None),
        P("cell", None),
    )

    return jax.shard_map(
        body,
        mesh=mesh,
        in_specs=placed,
        out_specs=P(None, "wide", "cell", None, None),
        check_vma=False,
    )
```

```python
from functools import partial
import math

import jax
import jax.numpy as jnp
from jax import lax
from jax.experimental import pallas as pl
from jax.experimental.pallas import tpu as pltpu
from jax.sharding import PartitionSpec as P


FORWARD = 4
BACKWARD = 3
TILE = 8
GRAIN = 16


def heights(order, parts):
    grains = order // GRAIN
    sizes = [grains // parts + (1 if k < grains % parts else 0) for k in range(parts)]
    return [s * GRAIN for s in sizes]


def starts_of(sizes):
    return [sum(sizes[:k]) for k in range(len(sizes))]


def waves(parts, stages):
    pairs = [(k, stage) for k in range(parts) for stage in stages]
    return sorted(pairs, key=lambda p: (p[0] + p[1], p[1]))


def bits_of(peers):
    return peers.bit_length() - 1


def own_bit(me, bit):
    return (me >> bit) & 1


def spin(pair, flag, turns):
    c, s = math.cos(2 * math.pi * turns), math.sin(2 * math.pi * turns)
    on = flag == 1
    re, im = pair
    return (jnp.where(on, c * re - s * im, re), jnp.where(on, c * im + s * re, im))


def phase(me, bits, low, unit, top=0):
    pair = (jnp.float32(1.0), jnp.float32(0.0))
    if top:
        angle = 2 * math.pi * unit * (top << bits)
        pair = (jnp.float32(math.cos(angle)), jnp.float32(math.sin(angle)))
    for s in range(low):
        pair = spin(pair, own_bit(me, bits - 1 - s), unit * (1 << s))
    return pair


def times(value, c, s):
    re, im = value
    return (c * re - s * im, c * im + s * re)


def dft(values, sign):
    count = len(values)
    if count == 1:
        return values
    even, odd = dft(values[0::2], sign), dft(values[1::2], sign)
    out = [None] * count
    for k in range(count // 2):
        re, im = odd[k]
        if k == 0:
            turned = (re, im)
        elif 4 * k == count:
            turned = (-im, re) if sign > 0 else (im, -re)
        else:
            angle = sign * 2 * math.pi * k / count
            turned = times(odd[k], math.cos(angle), math.sin(angle))
        out[k] = (even[k][0] + turned[0], even[k][1] + turned[1])
        out[k + count // 2] = (even[k][0] - turned[0], even[k][1] - turned[1])
    return out


def tiles_loop(rows, step):
    def run(i, carry):
        step(pl.ds(pl.multiple_of(i * TILE, TILE), TILE))
        return carry

    lax.fori_loop(0, rows // TILE, run, 0)


def call(kernel, outs, *args, smem=(), scratch=(), alias=None):
    specs = [
        pl.BlockSpec(memory_space=pltpu.SMEM if i in smem else pltpu.VMEM)
        for i in range(len(args))
    ]
    outs = [o if isinstance(o, jax.ShapeDtypeStruct) else full(o) for o in outs]
    nbytes = sum(a.size * a.dtype.itemsize for a in [*args, *outs, *map(full, scratch)])
    return pl.pallas_call(
        kernel,
        out_shape=outs,
        in_specs=specs,
        out_specs=[pl.BlockSpec(memory_space=pltpu.VMEM) for _ in outs],
        scratch_shapes=[pltpu.VMEM(shape, jnp.float32) for shape in scratch],
        input_output_aliases=alias or {},
        cost_estimate=pl.CostEstimate(flops=nbytes, bytes_accessed=nbytes, transcendentals=0),
        compiler_params=pltpu.CompilerParams(vmem_limit_bytes=nbytes + (4 << 20)),
    )(*args)


def full(shape):
    return jax.ShapeDtypeStruct(shape, jnp.float32)


def half(shape):
    return jax.ShapeDtypeStruct(shape, jnp.bfloat16)


def halves(value):
    high = value.astype(jnp.bfloat16)
    return high, (value - high.astype(jnp.float32)).astype(jnp.bfloat16)


def product_of(left, right):
    dot = partial(jnp.dot, preferred_element_type=jnp.float32)
    return dot(left[0], right[0]) + (dot(left[0], right[1]) + dot(left[1], right[0]))


def split_first(own, got, had):
    return jnp.where(had == 1, got, own), jnp.where(had == 1, own, got)


def forward_kernel(stage, bits, own_ref, got_ref, keep_ref, send_ref):
    me = lax.axis_index("wide")
    local, rows = own_ref.shape[2], own_ref.shape[3]
    had = own_bit(me, bits - stage)
    mine = own_bit(me, bits - 1 - stage)
    c, s = phase(me, bits, stage, 1.0 / (1 << (stage + 1)))
    flip = jnp.where(mine == 1, jnp.float32(-1.0), jnp.float32(1.0))
    c, s = c * flip, s * flip

    def step(at):
        for which in range(2):
            side = -s if which == 0 else s
            for j in range(local):
                pairs = [
                    split_first(own_ref[which, i, j, at], got_ref[which, i, j, at], had)
                    for i in range(2)
                ]
                turned = times((pairs[0][1], pairs[1][1]), c, side)
                for i in range(2):
                    keep_ref[which, i, j, at] = pairs[i][0] + turned[i]
                    send_ref[which, i, j, at] = pairs[i][0] - turned[i]

    tiles_loop(rows, step)


def product_kernel(bits, own_ref, got_ref, lesser_ref, polar_ref):
    me = lax.axis_index("wide")
    local, rows = own_ref.shape[2], own_ref.shape[3]
    peers = 1 << bits
    period = 2 * peers * local
    had = own_bit(me, 0)
    c, s = phase(me, bits, bits, 1.0 / (2 * peers))
    twist = [
        [phase(me, bits, bits, j / period, top) for j in range(local)] for top in range(2)
    ]

    def step(at):
        hats = []
        for which in range(2):
            sign = -1 if which == 0 else 1
            tops = [[], []]
            for j in range(local):
                pairs = [
                    split_first(own_ref[which, i, j, at], got_ref[which, i, j, at], had)
                    for i in range(2)
                ]
                turned = times((pairs[0][1], pairs[1][1]), c, sign * s)
                for top in range(2):
                    value = tuple(
                        pairs[i][0] + turned[i] if top == 0 else pairs[i][0] - turned[i]
                        for i in range(2)
                    )
                    if j > 0:
                        value = times(value, twist[top][j][0], sign * twist[top][j][1])
                    tops[top].append(value)
            hats.append(dft(tops[0], sign) + dft(tops[1], sign))
        for f in range(2 * local):
            a, b = hats[0][f], hats[1][f]
            lesser_ref[0, f, at], lesser_ref[1, f, at] = a
            polar_ref[0, f, at], polar_ref[1, f, at] = times(a, b[0], b[1])

    tiles_loop(rows, step)


def backward_kernel(bit, bits, sizes, own_ref, got_ref, *outs):
    me = lax.axis_index("wide")
    local = own_ref.shape[1]
    had, mine = own_bit(me, bit - 1), own_bit(me, bit)
    low = bits - bit
    c, s = phase(me, bits, low, 1.0 / (1 << (low + 1)))
    for k, (start, size) in enumerate(zip(starts_of(sizes), sizes)):
        keep_ref, send_ref = outs[2 * k], outs[2 * k + 1]

        def run(i, carry, start=start, keep_ref=keep_ref, send_ref=send_ref):
            to = pl.ds(pl.multiple_of(i * TILE, TILE), TILE)
            at = pl.ds(pl.multiple_of(start + i * TILE, TILE), TILE)
            for j in range(local):
                pairs = [
                    split_first(own_ref[p, j, at], got_ref[p, j, at], had) for p in range(2)
                ]
                total = [pairs[p][0] + pairs[p][1] for p in range(2)]
                gap = times([pairs[p][0] - pairs[p][1] for p in range(2)], c, s)
                for p in range(2):
                    keep_ref[p, j, to] = jnp.where(mine == 1, gap[p], total[p])
                    send_ref[p, j, to] = jnp.where(mine == 1, total[p], gap[p])
            return carry

        lax.fori_loop(0, size // TILE, run, 0)


def add_kernel(own_ref, got_ref, out_ref):
    out_ref[...] = own_ref[...] + got_ref[...]


def chosen(slots, at_zero, at_one):
    return jnp.where(slots[0], at_zero, 0.0) + jnp.where(slots[1], at_one, 0.0)


def places_of(row):
    side = 1 - 2 * (row & 1)
    return [0, side, -side]


def hits(offsets_ref, row, cells, place):
    inside = jnp.logical_and(row + place >= 0, row + place < cells)
    return [jnp.logical_and(inside, offsets_ref[0, j] == place) for j in range(2)]


def prepare_coulomb(scale, cells, offsets_ref, coulomb_ref, left_high, left_low, right_high, right_low):
    row = lax.axis_index("cell")
    order = coulomb_ref.shape[-1]
    for slot, place in enumerate(places_of(row)):
        hit = hits(offsets_ref, row, cells, place)
        value = chosen(hit, coulomb_ref[0, 0], coulomb_ref[0, 1])
        at = slice(slot * order, (slot + 1) * order)
        left_high[:, at], left_low[:, at] = halves(value)
        right_high[slot], right_low[slot] = halves(value.T * scale)


def prepare_green(cells, offsets_ref, green_ref, left_high, left_low, right_high, right_low):
    row = lax.axis_index("cell")
    local, order = green_ref.shape[1], green_ref.shape[-1]
    low, top = slice(0, order), slice(order, 2 * order)
    for slot, place in enumerate(places_of(row)):
        hit = hits(offsets_ref, row, cells, place)
        for e in range(local):
            parts = [chosen(hit, green_ref[i, e, 0, 0], green_ref[i, e, 0, 1]) for i in range(2)]
            for i, part in enumerate(parts):
                at = slice((2 * slot + i) * order, (2 * slot + i + 1) * order)
                left_high[e, :, at], left_low[e, :, at] = halves(part)
            re_t, im_t = (halves(p.T) for p in parts)
            for i, right in enumerate((right_high, right_low)):
                right[slot, e, low, low], right[slot, e, top, top] = re_t[i], re_t[i]
                right[slot, e, top, low], right[slot, e, low, top] = -im_t[i], im_t[i]


def screen_kernel(start, *refs):
    blocks, (right_high, right_low), (out_high, out_low) = refs[:3], refs[3:5], refs[-2:]
    count, rows, order = blocks[0].shape[1], blocks[0].shape[2], blocks[0].shape[3]
    for slot, ref in enumerate(blocks):
        value = halves(ref[...].reshape(2 * count * rows, order))
        result = halves(product_of(value, (right_high[slot], right_low[slot])))
        at = slice(slot * order + start, slot * order + start + rows)
        for out, value in zip((out_high, out_low), result):
            value = value.reshape(2, count, rows, order)
            for i in range(2):
                out[:, at, i * order : (i + 1) * order] = value[i]


def inverse_kernel(bits, sizes, *refs):
    me = lax.axis_index("wide")
    lesser_refs, refs = refs[: len(sizes)], refs[len(sizes) :]
    left_high, left_low, mid_high, mid_low, keep_ref, send_ref, screened = refs
    for f in range(mid_high.shape[0]):
        screened[f] = product_of((left_high[...], left_low[...]), (mid_high[f], mid_low[f]))
    local, order = keep_ref.shape[1], keep_ref.shape[-1]
    peers = 1 << bits
    period = 2 * peers * local
    mine = own_bit(me, 0)
    c, s = phase(me, bits, bits, 1.0 / (2 * peers))
    twist = [
        [phase(me, bits, bits, j / period, top) for j in range(local)] for top in range(2)
    ]
    for lesser_ref, start, size in zip(lesser_refs, starts_of(sizes), sizes):

        def run(k, carry, lesser_ref=lesser_ref, start=start):
            at = pl.ds(pl.multiple_of(k * TILE, TILE), TILE)
            to = pl.ds(pl.multiple_of(start + k * TILE, TILE), TILE)
            tops = []
            for top in range(2):
                values = []
                for t in range(local):
                    f = top * local + t
                    a = (lesser_ref[0, f, at], lesser_ref[1, f, at])
                    values.append(times(a, screened[f, to, :order], screened[f, to, order:]))
                values = dft(values, 1)
                tops.append(
                    [v if j == 0 else times(v, *twist[top][j]) for j, v in enumerate(values)]
                )
            for j in range(local):
                total = [tops[0][j][i] + tops[1][j][i] for i in range(2)]
                gap = times([tops[0][j][i] - tops[1][j][i] for i in range(2)], c, s)
                for i in range(2):
                    keep_ref[i, j, to] = jnp.where(mine == 1, gap[i], total[i])
                    send_ref[i, j, to] = jnp.where(mine == 1, total[i], gap[i])
            return carry

        lax.fori_loop(0, size // TILE, run, 0)


def times_right(block_ref, e, right_high, right_low, slot):
    value = halves(jnp.concatenate([block_ref[0, e], block_ref[1, e]], axis=-1))
    return product_of(value, (right_high[slot, e], right_low[slot, e]))


def own_dressing_kernel(count, *refs):
    blocks, (left_high, left_low, right_high, right_low, out_ref) = refs[:count], refs[count:]
    local, order = out_ref.shape[0], out_ref.shape[1]
    for e in range(local):
        parts = [times_right(b, e, right_high, right_low, 0) for b in blocks]
        value = jnp.concatenate(parts, axis=0)
        turned = jnp.concatenate([-value[:, order:], value[:, :order]], axis=-1)
        middle = halves(jnp.concatenate([value, turned], axis=0))
        out_ref[e] = product_of(
            (left_high[e, :, : 2 * order], left_low[e, :, : 2 * order]), middle
        )


def dress_kernel(start, *refs):
    blocks, (right_high, right_low), (out_high, out_low) = refs[:2], refs[2:4], refs[-2:]
    local, rows, order = blocks[0].shape[1], blocks[0].shape[2], blocks[0].shape[3]
    for slot, ref in enumerate(blocks):
        plain = slice(2 * slot * order + start, 2 * slot * order + start + rows)
        turned = slice((2 * slot + 1) * order + start, (2 * slot + 1) * order + start + rows)
        for e in range(local):
            result = halves(times_right(ref, e, right_high, right_low, slot + 1))
            for out, value in zip((out_high, out_low), result):
                out[e, plain] = value
                out[e, turned, :order], out[e, turned, order:] = -value[:, order:], value[:, :order]


def finish_kernel(own_ref, left_high, left_low, mid_high, mid_low, out_ref):
    local, order = out_ref.shape[1], out_ref.shape[-1]
    for e in range(local):
        total = own_ref[e] + product_of(
            (left_high[e, :, 2 * order :], left_low[e, :, 2 * order :]), (mid_high[e], mid_low[e])
        )
        out_ref[0, e, 0], out_ref[1, e, 0] = total[:, :order], total[:, order:]


def cut_kernel(starts, source_ref, *refs):
    outs, sems = refs[: len(starts)], refs[len(starts)]
    copies = [
        pltpu.make_async_copy(
            source_ref.at[:, :, :, 0, pl.ds(start, out.shape[3])], out, sems.at[k]
        )
        for k, (start, out) in enumerate(zip(starts, outs))
    ]
    for copy in copies:
        copy.start()
    for copy in copies:
        copy.wait()


def cut(value, starts, sizes):
    shapes = [full(value.shape[:3] + (size, value.shape[-1])) for size in sizes]
    return pl.pallas_call(
        partial(cut_kernel, starts),
        out_shape=shapes,
        in_specs=[pl.BlockSpec(memory_space=pl.ANY)],
        out_specs=[pl.BlockSpec(memory_space=pltpu.VMEM) for _ in shapes],
        scratch_shapes=[pltpu.SemaphoreType.DMA((len(shapes),))],
        compiler_params=pltpu.CompilerParams(
            vmem_limit_bytes=4 * sum(o.size for o in shapes) + (1 << 19)
        ),
    )(value)


def body(green_pair, coulomb, green_retarded, offsets):
    peers, cells = lax.axis_size("wide"), lax.axis_size("cell")
    local, order = green_pair.shape[2], green_pair.shape[-1]
    bits = bits_of(peers)
    energies = peers * local
    scale = 1.0 / (2 * energies * energies)

    def swap(value, bit):
        return lax.ppermute(value, "wide", [(i, i ^ (1 << bit)) for i in range(peers)])

    links = []
    for first in range(2):
        partner = list(range(cells))
        for i in range(first, cells - 1, 2):
            partner[i], partner[i + 1] = i + 1, i
        links.append(
            [
                (d * cells + c, (d ^ (c == partner[c])) * cells + partner[c])
                for d in range(peers) for c in range(cells)
            ]
        )

    def beside(value):
        blocks = []
        for pairs in links:
            blocks.append(lax.ppermute(value, ("wide", "cell"), pairs))
        return blocks

    sizes = heights(order, FORWARD)
    starts = starts_of(sizes)
    keep = [*cut(green_pair, starts[:1], sizes[:1]), *cut(green_pair, starts[1:], sizes[1:])]
    got = [swap(own, bits - 1) for own in keep]
    coulomb_shapes = [(order, 3 * order)] * 2 + [(3, order, order)] * 2
    coulombs = call(
        partial(prepare_coulomb, scale, cells), [half(c) for c in coulomb_shapes],
        offsets, coulomb, smem=(0,),
    )
    greens = call(
        partial(prepare_green, cells),
        [half((local, order, 6 * order))] * 2 + [half((3, local, 2 * order, 2 * order))] * 2,
        offsets, green_retarded, smem=(0,),
    )
    lesser, near = [None] * FORWARD, [None] * FORWARD
    for k, stage in waves(FORWARD, range(1, bits)):
        keep[k], send = call(
            partial(forward_kernel, stage, bits),
            [keep[k].shape] * 2, keep[k], got[k],
        )
        got[k] = swap(send, bits - 1 - stage)
        if stage == bits - 1:
            lesser[k], polar = call(
                partial(product_kernel, bits),
                [(2, 2 * local, sizes[k], order)] * 2, keep[k], got[k],
            )
            near[k] = [polar] + beside(polar)

    middle = []
    for k, start in enumerate(starts_of(sizes)):
        middle = call(
            partial(screen_kernel, start),
            [half((2 * local, 3 * order, 2 * order))] * 2, *near[k], *coulombs[2:], *middle,
            alias={5: 0, 6: 1} if k else None,
        )
    keep, send = call(
        partial(inverse_kernel, bits, sizes),
        [(2, local, order, order)] * 2, *lesser, *coulombs[:2], *middle,
        scratch=[(2 * local, order, 2 * order)],
    )
    got = swap(send, 0)
    sizes = heights(order, BACKWARD)
    outs = call(
        partial(backward_kernel, 1, bits, sizes),
        [(2, local, size, order) for size in sizes for _ in range(2)], keep, got,
    )
    keep = list(outs[0::2])
    got = [swap(send, 1) for send in outs[1::2]]
    near = [None] * BACKWARD
    for k, bit in waves(BACKWARD, range(2, bits + 1)):
        if bit < bits:
            keep[k], send = call(
                partial(backward_kernel, bit, bits, [sizes[k]]),
                [keep[k].shape] * 2, keep[k], got[k],
            )
            got[k] = swap(send, bit)
        else:
            sigma, = call(add_kernel, [keep[k].shape], keep[k], got[k])
            near[k] = [sigma] + beside(sigma)
    own, = call(
        partial(own_dressing_kernel, BACKWARD), [(local, order, 2 * order)],
        *[n[0] for n in near], *greens,
    )
    middle = []
    for k, start in enumerate(starts_of(sizes)):
        middle = call(
            partial(dress_kernel, start), [half((local, 4 * order, 2 * order))] * 2,
            *near[k][1:], *greens[2:], *middle, alias={4: 0, 5: 1} if k else None,
        )
    result, = call(finish_kernel, [(2, local, 1, order, order)], own, *greens[:2], *middle)
    return result


def solution(mesh):
    placed = (
        P(None, None, "wide", "cell", None, None),
        P("cell", None, None, None),
        P(None, "wide", "cell", None, None, None),
        P("cell", None),
    )

    return jax.shard_map(
        body,
        mesh=mesh,
        in_specs=placed,
        out_specs=P(None, "wide", "cell", None, None),
        check_vma=False,
    )
```

```python
from functools import partial
import math

import jax
import jax.numpy as jnp
from jax import lax
from jax.experimental import pallas as pl
from jax.experimental.pallas import tpu as pltpu
from jax.sharding import PartitionSpec as P


FORWARD = 4
BACKWARD = 3
TILE = 8
GRAIN = 16


def heights(order, parts):
    grains = order // GRAIN
    sizes = [grains // parts + (1 if k < grains % parts else 0) for k in range(parts)]
    return [s * GRAIN for s in sizes]


def starts_of(sizes):
    return [sum(sizes[:k]) for k in range(len(sizes))]


def waves(parts, stages):
    pairs = [(k, stage) for k in range(parts) for stage in stages]
    return sorted(pairs, key=lambda p: (p[0] + p[1], p[1]))


def bits_of(peers):
    return peers.bit_length() - 1


def own_bit(me, bit):
    return (me >> bit) & 1


def spin(pair, flag, turns):
    c, s = math.cos(2 * math.pi * turns), math.sin(2 * math.pi * turns)
    on = flag == 1
    re, im = pair
    return (jnp.where(on, c * re - s * im, re), jnp.where(on, c * im + s * re, im))


def phase(me, bits, low, unit, top=0):
    pair = (jnp.float32(1.0), jnp.float32(0.0))
    if top:
        angle = 2 * math.pi * unit * (top << bits)
        pair = (jnp.float32(math.cos(angle)), jnp.float32(math.sin(angle)))
    for s in range(low):
        pair = spin(pair, own_bit(me, bits - 1 - s), unit * (1 << s))
    return pair


def times(value, c, s):
    re, im = value
    return (c * re - s * im, c * im + s * re)


def dft(values, sign):
    count = len(values)
    if count == 1:
        return values
    even, odd = dft(values[0::2], sign), dft(values[1::2], sign)
    out = [None] * count
    for k in range(count // 2):
        re, im = odd[k]
        if k == 0:
            turned = (re, im)
        elif 4 * k == count:
            turned = (-im, re) if sign > 0 else (im, -re)
        else:
            angle = sign * 2 * math.pi * k / count
            turned = times(odd[k], math.cos(angle), math.sin(angle))
        out[k] = (even[k][0] + turned[0], even[k][1] + turned[1])
        out[k + count // 2] = (even[k][0] - turned[0], even[k][1] - turned[1])
    return out


def tiles_loop(rows, step):
    def run(i, carry):
        step(pl.ds(pl.multiple_of(i * TILE, TILE), TILE))
        return carry

    lax.fori_loop(0, rows // TILE, run, 0)


def call(kernel, outs, *args, smem=(), scratch=(), alias=None):
    specs = [
        pl.BlockSpec(memory_space=pltpu.SMEM if i in smem else pltpu.VMEM)
        for i in range(len(args))
    ]
    outs = [o if isinstance(o, jax.ShapeDtypeStruct) else full(o) for o in outs]
    nbytes = sum(a.size * a.dtype.itemsize for a in [*args, *outs, *map(full, scratch)])
    return pl.pallas_call(
        kernel,
        out_shape=outs,
        in_specs=specs,
        out_specs=[pl.BlockSpec(memory_space=pltpu.VMEM) for _ in outs],
        scratch_shapes=[pltpu.VMEM(shape, jnp.float32) for shape in scratch],
        input_output_aliases=alias or {},
        cost_estimate=pl.CostEstimate(flops=nbytes, bytes_accessed=nbytes, transcendentals=0),
        compiler_params=pltpu.CompilerParams(vmem_limit_bytes=nbytes + (4 << 20)),
    )(*args)


def full(shape):
    return jax.ShapeDtypeStruct(shape, jnp.float32)


def half(shape):
    return jax.ShapeDtypeStruct(shape, jnp.bfloat16)


def halves(value):
    high = value.astype(jnp.bfloat16)
    return high, (value - high.astype(jnp.float32)).astype(jnp.bfloat16)


def product_of(left, right):
    dot = partial(jnp.dot, preferred_element_type=jnp.float32)
    return dot(left[0], right[0]) + (dot(left[0], right[1]) + dot(left[1], right[0]))


def split_first(own, got, had):
    return jnp.where(had == 1, got, own), jnp.where(had == 1, own, got)


def forward_kernel(stage, bits, own_ref, got_ref, keep_ref, send_ref):
    me = lax.axis_index("wide")
    local, rows = own_ref.shape[2], own_ref.shape[3]
    had = own_bit(me, bits - stage)
    mine = own_bit(me, bits - 1 - stage)
    c, s = phase(me, bits, stage, 1.0 / (1 << (stage + 1)))
    flip = jnp.where(mine == 1, jnp.float32(-1.0), jnp.float32(1.0))
    c, s = c * flip, s * flip

    def step(at):
        for which in range(2):
            side = -s if which == 0 else s
            for j in range(local):
                pairs = [
                    split_first(own_ref[which, i, j, at], got_ref[which, i, j, at], had)
                    for i in range(2)
                ]
                turned = times((pairs[0][1], pairs[1][1]), c, side)
                for i in range(2):
                    keep_ref[which, i, j, at] = pairs[i][0] + turned[i]
                    send_ref[which, i, j, at] = pairs[i][0] - turned[i]

    tiles_loop(rows, step)


def product_kernel(bits, own_ref, got_ref, lesser_ref, polar_ref):
    me = lax.axis_index("wide")
    local, rows = own_ref.shape[2], own_ref.shape[3]
    peers = 1 << bits
    period = 2 * peers * local
    had = own_bit(me, 0)
    c, s = phase(me, bits, bits, 1.0 / (2 * peers))
    twist = [
        [phase(me, bits, bits, j / period, top) for j in range(local)] for top in range(2)
    ]

    def step(at):
        hats = []
        for which in range(2):
            sign = -1 if which == 0 else 1
            tops = [[], []]
            for j in range(local):
                pairs = [
                    split_first(own_ref[which, i, j, at], got_ref[which, i, j, at], had)
                    for i in range(2)
                ]
                turned = times((pairs[0][1], pairs[1][1]), c, sign * s)
                for top in range(2):
                    value = tuple(
                        pairs[i][0] + turned[i] if top == 0 else pairs[i][0] - turned[i]
                        for i in range(2)
                    )
                    if j > 0:
                        value = times(value, twist[top][j][0], sign * twist[top][j][1])
                    tops[top].append(value)
            hats.append(dft(tops[0], sign) + dft(tops[1], sign))
        for f in range(2 * local):
            a, b = hats[0][f], hats[1][f]
            lesser_ref[0, f, at], lesser_ref[1, f, at] = a
            polar_ref[0, f, at], polar_ref[1, f, at] = times(a, b[0], b[1])

    tiles_loop(rows, step)


def backward_kernel(bit, bits, sizes, own_ref, got_ref, *outs):
    me = lax.axis_index("wide")
    local = own_ref.shape[1]
    had, mine = own_bit(me, bit - 1), own_bit(me, bit)
    low = bits - bit
    c, s = phase(me, bits, low, 1.0 / (1 << (low + 1)))
    for k, (start, size) in enumerate(zip(starts_of(sizes), sizes)):
        keep_ref, send_ref = outs[2 * k], outs[2 * k + 1]

        def run(i, carry, start=start, keep_ref=keep_ref, send_ref=send_ref):
            to = pl.ds(pl.multiple_of(i * TILE, TILE), TILE)
            at = pl.ds(pl.multiple_of(start + i * TILE, TILE), TILE)
            for j in range(local):
                pairs = [
                    split_first(own_ref[p, j, at], got_ref[p, j, at], had) for p in range(2)
                ]
                total = [pairs[p][0] + pairs[p][1] for p in range(2)]
                gap = times([pairs[p][0] - pairs[p][1] for p in range(2)], c, s)
                for p in range(2):
                    keep_ref[p, j, to] = jnp.where(mine == 1, gap[p], total[p])
                    send_ref[p, j, to] = jnp.where(mine == 1, total[p], gap[p])
            return carry

        lax.fori_loop(0, size // TILE, run, 0)


def add_kernel(own_ref, got_ref, out_ref):
    out_ref[...] = own_ref[...] + got_ref[...]


def chosen(slots, at_zero, at_one):
    return jnp.where(slots[0], at_zero, 0.0) + jnp.where(slots[1], at_one, 0.0)


def places_of(row):
    side = 1 - 2 * (row & 1)
    return [0, side, -side]


def hits(offsets_ref, row, cells, place):
    inside = jnp.logical_and(row + place >= 0, row + place < cells)
    return [jnp.logical_and(inside, offsets_ref[0, j] == place) for j in range(2)]


def prepare_coulomb(scale, cells, offsets_ref, coulomb_ref, left_high, left_low, right_high, right_low):
    row = lax.axis_index("cell")
    order = coulomb_ref.shape[-1]
    for slot, place in enumerate(places_of(row)):
        hit = hits(offsets_ref, row, cells, place)
        value = chosen(hit, coulomb_ref[0, 0], coulomb_ref[0, 1])
        at = slice(slot * order, (slot + 1) * order)
        left_high[:, at], left_low[:, at] = halves(value)
        right_high[slot], right_low[slot] = halves(value.T * scale)


def prepare_green(cells, offsets_ref, green_ref, left_high, left_low, right_high, right_low):
    row = lax.axis_index("cell")
    local, order = green_ref.shape[1], green_ref.shape[-1]
    low, top = slice(0, order), slice(order, 2 * order)
    for slot, place in enumerate(places_of(row)):
        hit = hits(offsets_ref, row, cells, place)
        for e in range(local):
            parts = [chosen(hit, green_ref[i, e, 0, 0], green_ref[i, e, 0, 1]) for i in range(2)]
            for i, part in enumerate(parts):
                at = slice((2 * slot + i) * order, (2 * slot + i + 1) * order)
                left_high[e, :, at], left_low[e, :, at] = halves(part)
            re_t, im_t = (halves(p.T) for p in parts)
            for i, right in enumerate((right_high, right_low)):
                right[slot, e, low, low], right[slot, e, top, top] = re_t[i], re_t[i]
                right[slot, e, top, low], right[slot, e, low, top] = -im_t[i], im_t[i]


def screen_kernel(start, *refs):
    blocks, (right_high, right_low), (out_high, out_low) = refs[:3], refs[3:5], refs[-2:]
    count, rows, order = blocks[0].shape[1], blocks[0].shape[2], blocks[0].shape[3]
    for slot, ref in enumerate(blocks):
        value = halves(ref[...].reshape(2 * count * rows, order))
        result = halves(product_of(value, (right_high[slot], right_low[slot])))
        at = slice(slot * order + start, slot * order + start + rows)
        for out, value in zip((out_high, out_low), result):
            value = value.reshape(2, count, rows, order)
            for i in range(2):
                out[:, at, i * order : (i + 1) * order] = value[i]


def inverse_kernel(bits, sizes, *refs):
    me = lax.axis_index("wide")
    lesser_refs, refs = refs[: len(sizes)], refs[len(sizes) :]
    left_high, left_low, mid_high, mid_low, keep_ref, send_ref, screened = refs
    for f in range(mid_high.shape[0]):
        screened[f] = product_of((left_high[...], left_low[...]), (mid_high[f], mid_low[f]))
    local, order = keep_ref.shape[1], keep_ref.shape[-1]
    peers = 1 << bits
    period = 2 * peers * local
    mine = own_bit(me, 0)
    c, s = phase(me, bits, bits, 1.0 / (2 * peers))
    twist = [
        [phase(me, bits, bits, j / period, top) for j in range(local)] for top in range(2)
    ]
    for lesser_ref, start, size in zip(lesser_refs, starts_of(sizes), sizes):

        def run(k, carry, lesser_ref=lesser_ref, start=start):
            at = pl.ds(pl.multiple_of(k * TILE, TILE), TILE)
            to = pl.ds(pl.multiple_of(start + k * TILE, TILE), TILE)
            tops = []
            for top in range(2):
                values = []
                for t in range(local):
                    f = top * local + t
                    a = (lesser_ref[0, f, at], lesser_ref[1, f, at])
                    values.append(times(a, screened[f, to, :order], screened[f, to, order:]))
                values = dft(values, 1)
                tops.append(
                    [v if j == 0 else times(v, *twist[top][j]) for j, v in enumerate(values)]
                )
            for j in range(local):
                total = [tops[0][j][i] + tops[1][j][i] for i in range(2)]
                gap = times([tops[0][j][i] - tops[1][j][i] for i in range(2)], c, s)
                for i in range(2):
                    keep_ref[i, j, to] = jnp.where(mine == 1, gap[i], total[i])
                    send_ref[i, j, to] = jnp.where(mine == 1, total[i], gap[i])
            return carry

        lax.fori_loop(0, size // TILE, run, 0)


def times_right(block_ref, e, right_high, right_low, slot):
    value = halves(jnp.concatenate([block_ref[0, e], block_ref[1, e]], axis=-1))
    return product_of(value, (right_high[slot, e], right_low[slot, e]))


def own_dressing_kernel(count, *refs):
    blocks, (left_high, left_low, right_high, right_low, out_ref) = refs[:count], refs[count:]
    local, order = out_ref.shape[0], out_ref.shape[1]
    for e in range(local):
        parts = [times_right(b, e, right_high, right_low, 0) for b in blocks]
        value = jnp.concatenate(parts, axis=0)
        turned = jnp.concatenate([-value[:, order:], value[:, :order]], axis=-1)
        middle = halves(jnp.concatenate([value, turned], axis=0))
        out_ref[e] = product_of(
            (left_high[e, :, : 2 * order], left_low[e, :, : 2 * order]), middle
        )


def dress_kernel(start, *refs):
    blocks, (right_high, right_low), (out_high, out_low) = refs[:2], refs[2:4], refs[-2:]
    local, rows, order = blocks[0].shape[1], blocks[0].shape[2], blocks[0].shape[3]
    for slot, ref in enumerate(blocks):
        plain = slice(2 * slot * order + start, 2 * slot * order + start + rows)
        turned = slice((2 * slot + 1) * order + start, (2 * slot + 1) * order + start + rows)
        for e in range(local):
            result = halves(times_right(ref, e, right_high, right_low, slot + 1))
            for out, value in zip((out_high, out_low), result):
                out[e, plain] = value
                out[e, turned, :order], out[e, turned, order:] = -value[:, order:], value[:, :order]


def finish_kernel(own_ref, left_high, left_low, mid_high, mid_low, out_ref):
    local, order = out_ref.shape[1], out_ref.shape[-1]
    for e in range(local):
        total = own_ref[e] + product_of(
            (left_high[e, :, 2 * order :], left_low[e, :, 2 * order :]), (mid_high[e], mid_low[e])
        )
        out_ref[0, e, 0], out_ref[1, e, 0] = total[:, :order], total[:, order:]


def cut_kernel(starts, source_ref, *refs):
    outs, sems = refs[: len(starts)], refs[len(starts)]
    copies = [
        pltpu.make_async_copy(
            source_ref.at[:, :, :, 0, pl.ds(start, out.shape[3])], out, sems.at[k]
        )
        for k, (start, out) in enumerate(zip(starts, outs))
    ]
    for copy in copies:
        copy.start()
    for copy in copies:
        copy.wait()


def cut(value, starts, sizes):
    shapes = [full(value.shape[:3] + (size, value.shape[-1])) for size in sizes]
    return pl.pallas_call(
        partial(cut_kernel, starts),
        out_shape=shapes,
        in_specs=[pl.BlockSpec(memory_space=pl.ANY)],
        out_specs=[pl.BlockSpec(memory_space=pltpu.VMEM) for _ in shapes],
        scratch_shapes=[pltpu.SemaphoreType.DMA((len(shapes),))],
        compiler_params=pltpu.CompilerParams(
            vmem_limit_bytes=4 * sum(o.size for o in shapes) + (1 << 19)
        ),
    )(value)


def body(green_pair, coulomb, green_retarded, offsets):
    peers, cells = lax.axis_size("wide"), lax.axis_size("cell")
    local, order = green_pair.shape[2], green_pair.shape[-1]
    bits = bits_of(peers)
    energies = peers * local
    scale = 1.0 / (2 * energies * energies)

    def swap(value, bit):
        return lax.ppermute(value, "wide", [(i, i ^ (1 << bit)) for i in range(peers)])

    links = []
    for first in range(2):
        partner = list(range(cells))
        for i in range(first, cells - 1, 2):
            partner[i], partner[i + 1] = i + 1, i
        links.append(
            [
                (d * cells + c, (d ^ (c == partner[c])) * cells + partner[c])
                for d in range(peers) for c in range(cells)
            ]
        )

    def beside(value):
        blocks = []
        for pairs in links:
            blocks.append(lax.ppermute(value, ("wide", "cell"), pairs))
        return blocks

    sizes = heights(order, FORWARD)
    starts = starts_of(sizes)
    keep = [
        lax.slice_in_dim(green_pair[:, :, :, 0], 0, sizes[0], axis=3),
        *cut(green_pair, starts[1:], sizes[1:]),
    ]
    got = [swap(own, bits - 1) for own in keep]
    coulomb_shapes = [(order, 3 * order)] * 2 + [(3, order, order)] * 2
    coulombs = call(
        partial(prepare_coulomb, scale, cells), [half(c) for c in coulomb_shapes],
        offsets, coulomb, smem=(0,),
    )
    greens = call(
        partial(prepare_green, cells),
        [half((local, order, 6 * order))] * 2 + [half((3, local, 2 * order, 2 * order))] * 2,
        offsets, green_retarded, smem=(0,),
    )
    lesser, near = [None] * FORWARD, [None] * FORWARD
    for k, stage in waves(FORWARD, range(1, bits)):
        keep[k], send = call(
            partial(forward_kernel, stage, bits),
            [keep[k].shape] * 2, keep[k], got[k],
        )
        got[k] = swap(send, bits - 1 - stage)
        if stage == bits - 1:
            lesser[k], polar = call(
                partial(product_kernel, bits),
                [(2, 2 * local, sizes[k], order)] * 2, keep[k], got[k],
            )
            near[k] = [polar] + beside(polar)

    middle = []
    for k, start in enumerate(starts_of(sizes)):
        middle = call(
            partial(screen_kernel, start),
            [half((2 * local, 3 * order, 2 * order))] * 2, *near[k], *coulombs[2:], *middle,
            alias={5: 0, 6: 1} if k else None,
        )
    keep, send = call(
        partial(inverse_kernel, bits, sizes),
        [(2, local, order, order)] * 2, *lesser, *coulombs[:2], *middle,
        scratch=[(2 * local, order, 2 * order)],
    )
    got = swap(send, 0)
    sizes = heights(order, BACKWARD)
    outs = call(
        partial(backward_kernel, 1, bits, sizes),
        [(2, local, size, order) for size in sizes for _ in range(2)], keep, got,
    )
    keep = list(outs[0::2])
    got = [swap(send, 1) for send in outs[1::2]]
    near = [None] * BACKWARD
    for k, bit in waves(BACKWARD, range(2, bits + 1)):
        if bit < bits:
            keep[k], send = call(
                partial(backward_kernel, bit, bits, [sizes[k]]),
                [keep[k].shape] * 2, keep[k], got[k],
            )
            got[k] = swap(send, bit)
        else:
            sigma, = call(add_kernel, [keep[k].shape], keep[k], got[k])
            near[k] = [sigma] + beside(sigma)
    own, = call(
        partial(own_dressing_kernel, BACKWARD), [(local, order, 2 * order)],
        *[n[0] for n in near], *greens,
    )
    middle = []
    for k, start in enumerate(starts_of(sizes)):
        middle = call(
            partial(dress_kernel, start), [half((local, 4 * order, 2 * order))] * 2,
            *near[k][1:], *greens[2:], *middle, alias={4: 0, 5: 1} if k else None,
        )
    result, = call(finish_kernel, [(2, local, 1, order, order)], own, *greens[:2], *middle)
    return result


def solution(mesh):
    placed = (
        P(None, None, "wide", "cell", None, None),
        P("cell", None, None, None),
        P(None, "wide", "cell", None, None, None),
        P("cell", None),
    )

    return jax.shard_map(
        body,
        mesh=mesh,
        in_specs=placed,
        out_specs=P(None, "wide", "cell", None, None),
        check_vma=False,
    )
```
